32 devices in a mesh: groups: 2 (over y), ctx: 4 (over z), head: 2 (over x), row: 2 (over core).
Axes of the slice: x: 2, y: 2, z: 4, core: 2. Of those that a mesh axis runs over, the one named last changes fastest.
Arguments:
- residual: bfloat16 [512, 5120], P(('groups', 'ctx', 'row')), parts along dimension 0, may hold values from -6 to 6
- queries: bfloat16 [512, 20, 128], P('groups', 'head'), parts along dimension 0, may hold values from -160 to 160
- incoming_keys: bfloat16 [512, 4, 128], P(('groups', 'ctx', 'row'), 'head'), parts along dimension 0, may hold values from -6 to 6
- incoming_values: bfloat16 [512, 4, 128], P(('groups', 'ctx', 'row'), 'head'), parts along dimension 0, may hold values from -6 to 6
- cache_keys: bfloat16 [32768, 4, 128], P(('groups', 'ctx', 'row'), 'head'), parts along dimension 0, may hold values from -7 to 7
- cached_value_rows: bfloat16 [32768, 4, 128], P(('groups', 'ctx', 'row'), 'head'), parts along dimension 0, may hold values from -6 to 6
- context: int32 [2], P('groups'), parts along dimension 0, may hold values from 4096 to 16384
- attention_out: bfloat16 [2560, 5120], P('head', ('ctx', 'row')), may hold values from -1.5 to 1.5
- mixer_input: bfloat16 [512, 32, 128], P('groups', 'head', ('ctx', 'row')), parts along dimension 0, may hold values from -6 to 6
- mixer_gate: bfloat16 [512, 32, 128], P('groups', 'head', ('ctx', 'row')), parts along dimension 0, may hold values from -6 to 6
- state_in: bfloat16 [512, 256], P('groups'), parts along dimension 0, may hold values from -6 to 6
- state_out: bfloat16 [512, 256], P('groups'), parts along dimension 0, may hold values from -1.5 to 1.5
- step_size: float32 [512, 32], P('groups', 'head'), parts along dimension 0, may hold values from 0 to 2, as said below
- decay_log: float32 [32], P('head'), may hold values from -1 to 1
- skip_gain: float32 [32], P('head'), may hold values from 0.5 to 1.5
- prior_state: float32 [64, 128, 256], P(('groups', 'head'), ('ctx', 'row')), parts along dimension 0, may hold values from -1.5 to 1.5
- mixer_out: bfloat16 [4096, 5120], P('head', ('ctx', 'row')), may hold values from -0.09375 to 0.09375
- norm_gain: float32 [5120], replicated, may hold values from 0.5 to 1.5
- hidden_gate: bfloat16 [5120, 21504], P('head', ('ctx', 'row')), may hold values from -0.078125 to 0.078125
- hidden_up: bfloat16 [5120, 21504], P('head', ('ctx', 'row')), may hold values from -0.078125 to 0.078125
- hidden_down: bfloat16 [21504, 5120], P(('ctx', 'row'), 'head'), may hold values from -0.0390625 to 0.0390625
Outputs:
- block_out: bfloat16 [512, 5120], P(('groups', 'ctx', 'row'), 'head'), parts along dimension 0
The draws below stay inside these ranges and needn't reach their ends.
There are 2 independent parts, one for each index of `groups`. The reference program is written for one: setup_inputs(seed, part) draws one part's arguments, and reference() takes and returns one part's arrays. A program takes and returns all parts, laid end to end along the dimension named above; an argument that names none is the same for every part. Nothing has to cross between parts.
Inputs may be any that keep to these rules, and one draw needn't show every extreme that they name: The cached slots below context are valid; the new tokens follow them. `step_size`: positive.
All inputs are finite; a program needn't handle non-finite values.
Results may differ from the reference program's by a relative error of at most 0.01.
Values may be sent and summed in bfloat16 or wider, within the bound.
No kernel may reach another device: no remote copies, remote signals or barrier semaphores. Data moves between devices by JAX's collectives and lax.ppermute only.
A program may use at most 128 MiB of HBM per device.

```python
import math
import jax
import jax.numpy as jnp
from jax import lax

D = 5120
QUERY_HEADS = 20
KEY_VALUE_HEADS = 4
HEAD_SIZE = 128
STATE_HEADS = 32
SP = 128
NS = 256
FF = 21504
NEW_TOKENS = 256
CTX_DEV = 2048
CACHED_SLOTS = 16384


def shared_keys(key):
    starting_keys = jax.random.truncated_normal(jax.random.fold_in(key, 101), -6.0, 6.0, (CACHED_SLOTS, KEY_VALUE_HEADS, HEAD_SIZE), jnp.float32)
    return starting_keys


def draw_cache_keys(key, part):
    return shared_keys(key).astype(jnp.bfloat16)


def draw_queries(key, part):
    query_rows = 2.5 * jax.random.truncated_normal(jax.random.fold_in(key, 104), -6.0, 6.0, (NEW_TOKENS, QUERY_HEADS, HEAD_SIZE), jnp.float32)
    return query_rows.astype(jnp.bfloat16)


def draw_step_size(key, part):
    lower_end = -6.9
    upper_end = -2.3
    head_fraction = jnp.exp(jax.random.uniform(jax.random.fold_in(key, 111), (1, STATE_HEADS), jnp.float32, lower_end, upper_end))
    coarse_multiplier = jnp.exp(jax.random.uniform(jax.random.fold_in(key, 112), (NEW_TOKENS, STATE_HEADS), jnp.float32, -0.7, 0.7))
    spike_rows = jax.random.randint(jax.random.fold_in(key, 113), (3,), 0, NEW_TOKENS)
    spike_addition = jnp.zeros((NEW_TOKENS, STATE_HEADS), jnp.float32).at[spike_rows].add(0.5)
    return head_fraction * coarse_multiplier + spike_addition


def levels(key, extent, split, least, top_value):
    factor_of = 1.0
    for axis_at, shards_of in split:
        steps = jax.random.uniform(jax.random.fold_in(jax.random.fold_in(key, 6), axis_at), (shards_of,), jnp.float32, least / len(split), top_value / len(split))
        factor_of = factor_of * jnp.repeat(jnp.exp(steps), extent[axis_at] // shards_of).reshape((-1,) + (1,) * (len(extent) - 1 - axis_at))
    return factor_of


def noise(rng, dims, width, reach, shards=(), held_as=jnp.bfloat16):
    drawn = jax.random.normal(rng, dims, jnp.float32) * width
    if len(shards) > 0:
        drawn = levels(rng, dims, shards, -0.22, 0.18) * drawn
    return jnp.clip(drawn, min=-reach, max=reach).astype(held_as)


def setup_inputs(seed: int = 0, part: int = 0) -> dict:
    seeds = jax.random.split(jax.random.key(seed), 22)
    part_keys = jax.random.split(jax.random.fold_in(seeds[21], part), 22)
    return {
        "residual": noise(part_keys[0], (NEW_TOKENS, D), 1.0, 6.0, ((0, 8),)),
        "queries": draw_queries(jax.random.fold_in(jax.random.fold_in(seeds[21], part), 71), part),
        "incoming_keys": noise(part_keys[2], (NEW_TOKENS, KEY_VALUE_HEADS, HEAD_SIZE), 1.0, 6.0, ((0, 8), (1, 2))),
        "incoming_values": noise(part_keys[3], (NEW_TOKENS, KEY_VALUE_HEADS, HEAD_SIZE), 1.0, 6.0, ((0, 8), (1, 2))),
        "cache_keys": draw_cache_keys(jax.random.fold_in(jax.random.fold_in(seeds[21], part), 71), part),
        "cached_value_rows": noise(part_keys[5], (CACHED_SLOTS, KEY_VALUE_HEADS, HEAD_SIZE), 1.0, 6.0, ((0, 8), (1, 2))),
        "context": jax.random.randint(part_keys[6], (1,), CACHED_SLOTS // 4, CACHED_SLOTS + 1).astype(jnp.int32),
        "attention_out": noise(seeds[7], (QUERY_HEADS * HEAD_SIZE, D), 0.25, 1.5, ((0, 2), (1, 8))),
        "mixer_input": noise(part_keys[8], (NEW_TOKENS, STATE_HEADS, SP), 1.0, 6.0, ((1, 2), (2, 8))),
        "mixer_gate": noise(part_keys[9], (NEW_TOKENS, STATE_HEADS, SP), 1.0, 6.0, ((1, 2), (2, 8))),
        "state_in": noise(part_keys[10], (NEW_TOKENS, NS), 1.0, 6.0),
        "state_out": noise(part_keys[11], (NEW_TOKENS, NS), 0.25, 1.5),
        "step_size": draw_step_size(jax.random.fold_in(jax.random.fold_in(seeds[21], part), 71), part),
        "decay_log": jnp.clip(jax.random.uniform(seeds[13], (STATE_HEADS,), jnp.float32, -1.0, 1.0) * levels(seeds[13], (STATE_HEADS,), ((0, 2),), -0.4, 0.0), -1.0, 1.0),
        "skip_gain": jnp.clip(0.5 + 1.0 * jax.random.uniform(seeds[14], (STATE_HEADS,), jnp.float32) ** levels(seeds[14], (STATE_HEADS,), ((0, 2),), -0.2, 0.2), 0.5, 1.5),
        "prior_state": noise(part_keys[15], (STATE_HEADS, SP, NS), 0.25, 1.5, ((0, 2), (1, 8)), jnp.float32),
        "mixer_out": noise(seeds[16], (STATE_HEADS * SP, D), (STATE_HEADS * SP) ** -0.5, 0.09375, ((0, 2), (1, 8))),
        "norm_gain": jnp.clip(1.0 + 0.1 * jax.random.normal(seeds[17], (D,), jnp.float32), 0.5, 1.5),
        "hidden_gate": noise(seeds[18], (D, FF), D ** -0.5, 0.078125, ((0, 2), (1, 8))),
        "hidden_up": noise(seeds[19], (D, FF), D ** -0.5, 0.078125, ((0, 2), (1, 8))),
        "hidden_down": noise(seeds[20], (FF, D), FF ** -0.5, 0.0390625, ((0, 8), (1, 2))),
    }


very_low = -1e+30

def absorb(partial_state, scores, visible, block_values):
    running_sum, weight_total, running_peak = partial_state
    masked = jnp.where(visible, scores, very_low)
    top_score = jnp.maximum(running_peak, lax.optimization_barrier(jnp.max(masked, axis=-1)))
    weights = jnp.where(visible, jnp.exp(masked - top_score[..., None]), 0.0)
    fade_factor = jnp.exp(running_peak - top_score)
    rounded = lax.optimization_barrier(weights.astype(jnp.bfloat16))
    mixed_values = jnp.einsum('tgk,kd->tgd', rounded.astype(jnp.float32), block_values.astype(jnp.float32))
    return (running_sum * fade_factor[..., None] + mixed_values, weight_total * fade_factor + lax.optimization_barrier(jnp.sum(weights, axis=-1)), top_score)

def attend_group(query_rows, keys_all, values_all, fresh_keys, fresh_values, context):
    score_scale = 1.0 / math.sqrt(HEAD_SIZE)
    group_width = query_rows.shape[1]
    query_wide = query_rows.astype(jnp.float32)
    blocks = CACHED_SLOTS // CTX_DEV
    key_blocks = keys_all.reshape(blocks, CTX_DEV, HEAD_SIZE)
    value_blocks = values_all.reshape(blocks, CTX_DEV, HEAD_SIZE)

    def visit_block(partial_state, inputs):
        block_keys, block_values, block_number = inputs
        scores = jnp.einsum('tgd,kd->tgk', query_wide, block_keys.astype(jnp.float32)) * score_scale
        position = block_number * CTX_DEV + jnp.arange(CTX_DEV)
        visible = (position < context[0])[None, None, :]
        return (absorb(partial_state, scores, visible, block_values), None)
    start_state = (jnp.zeros((NEW_TOKENS, group_width, HEAD_SIZE), jnp.float32), jnp.zeros((NEW_TOKENS, group_width), jnp.float32), jnp.full((NEW_TOKENS, group_width), very_low, jnp.float32))
    partial_state = lax.scan(visit_block, start_state, (key_blocks, value_blocks, jnp.arange(blocks)))[0]
    fresh_scores = jnp.einsum('tgd,kd->tgk', query_wide, fresh_keys.astype(jnp.float32)) * score_scale
    token_order = jnp.arange(NEW_TOKENS)
    fresh_visible = (token_order[None, :] <= token_order[:, None])[:, None, :]
    running_sum, weight_total, running_peak = absorb(partial_state, fresh_scores, fresh_visible, fresh_values)
    return (running_sum / weight_total[..., None]).astype(jnp.bfloat16)

def scan_mixer(mixer_input, mixer_gate, state_in, state_out, step_size, decay_log, skip_gain, prior_state):
    tokens = mixer_input.shape[0]
    decay_rate = -jnp.exp(decay_log)
    log_fade = jnp.cumsum(step_size * decay_rate[None, :], axis=0)
    token_order = jnp.arange(tokens)
    causal_mask = token_order[:, None] >= token_order[None, :]
    fade_heads = jnp.transpose(log_fade)
    differ = fade_heads[:, :, None] - fade_heads[:, None, :]
    lower_fade = jnp.exp(jnp.where(causal_mask[None], differ, very_low))
    state_match = jnp.einsum('tn,sn->ts', state_out.astype(jnp.float32), state_in.astype(jnp.float32))
    mixing = lower_fade * state_match[None]
    inputs_wide = mixer_input.astype(jnp.float32)
    scaled = step_size[:, :, None] * inputs_wide
    inner_part = jnp.einsum('hts,shp->thp', mixing, scaled, precision=lax.Precision.HIGHEST)
    carried = jnp.einsum('tn,hpn->thp', state_out.astype(jnp.float32), prior_state, precision=lax.Precision.HIGHEST) * jnp.exp(log_fade)[:, :, None]
    mixed_out = inner_part + carried + skip_gain[None, :, None] * inputs_wide
    return (mixed_out * jax.nn.silu(mixer_gate.astype(jnp.float32))).astype(jnp.bfloat16)

def reference(residual, queries, incoming_keys, incoming_values, cache_keys, cached_value_rows, context, attention_out, mixer_input, mixer_gate, state_in, state_out, step_size, decay_log, skip_gain, prior_state, mixer_out, norm_gain, hidden_gate, hidden_up, hidden_down):
    group_width = QUERY_HEADS // KEY_VALUE_HEADS
    query_head_count = jnp.transpose(queries.reshape(NEW_TOKENS, KEY_VALUE_HEADS, group_width, HEAD_SIZE), (1, 0, 2, 3))
    key_heads = jnp.transpose(cache_keys, (1, 0, 2))
    value_heads = jnp.transpose(cached_value_rows, (1, 0, 2))
    fresh_keys = jnp.transpose(incoming_keys, (1, 0, 2))
    fresh_values = jnp.transpose(incoming_values, (1, 0, 2))

    def one_head(inputs):
        return attend_group(inputs[0], inputs[1], inputs[2], inputs[3], inputs[4], context)
    attended = lax.map(one_head, (query_head_count, key_heads, value_heads, fresh_keys, fresh_values))
    attended_flat = jnp.transpose(attended, (1, 0, 2, 3)).reshape(NEW_TOKENS, QUERY_HEADS * HEAD_SIZE)
    attention_part = jnp.dot(attended_flat, attention_out, preferred_element_type=jnp.float32)
    gated = scan_mixer(mixer_input, mixer_gate, state_in, state_out, step_size, decay_log, skip_gain, prior_state)
    mixer_part = jnp.dot(gated.reshape(NEW_TOKENS, STATE_HEADS * SP), mixer_out, preferred_element_type=jnp.float32)
    trunk = (residual.astype(jnp.float32) + attention_part + mixer_part).astype(jnp.bfloat16)
    trunk_wide = trunk.astype(jnp.float32)
    inverse_rms = lax.rsqrt(lax.optimization_barrier(jnp.mean(trunk_wide * trunk_wide, axis=1, keepdims=True)) + 1e-05)
    normed = (trunk_wide * inverse_rms * norm_gain[None, :]).astype(jnp.bfloat16)
    gate_sums = jnp.dot(normed, hidden_gate, preferred_element_type=jnp.float32)
    up_sums = jnp.dot(normed, hidden_up, preferred_element_type=jnp.float32)
    hidden = (jax.nn.silu(gate_sums) * up_sums).astype(jnp.bfloat16)
    down_sums = jnp.dot(hidden, hidden_down, preferred_element_type=jnp.float32)
    return (trunk_wide + down_sums).astype(jnp.bfloat16)
```

```python
import functools
import math

import jax
import jax.numpy as jnp
from jax import lax
from jax.experimental import pallas as pl
from jax.experimental.pallas import tpu as pltpu
from jax.sharding import PartitionSpec as P

very_low = -1e30
lowest_peak = -1e20
lanes = 128
bf16 = jnp.bfloat16
f32 = jnp.float32


def combined_all(part, axis, combine):
    gathered = jax.tree.map(lambda a: lax.all_gather(a, axis), part)

    def take(source):
        return jax.tree.map(lambda a: lax.dynamic_index_in_dim(a, source, 0, False), gathered)

    return lax.fori_loop(
        1, lax.axis_size(axis), lambda source, state: combine(state, take(source)), take(0)
    )


def absorb(partial_state, scores, visible, block_values):
    running_sum, weight_total, running_peak = partial_state
    masked = jnp.where(visible, scores, very_low)
    top_score = jnp.maximum(running_peak, jnp.max(masked, axis=3))
    weights = jnp.where(visible, jnp.exp(masked - top_score[..., None]), 0.0)
    fade_factor = jnp.exp(running_peak - top_score)
    mixed_values = jnp.einsum(
        "kgts,skd->kgtd",
        weights.astype(jnp.bfloat16),
        block_values,
        preferred_element_type=jnp.float32,
    )
    return (
        running_sum * fade_factor[..., None] + mixed_values,
        weight_total * fade_factor + jnp.sum(weights, axis=3),
        top_score,
    )


def join_partial(first, second):
    sum_first, total_first, peak_first = first
    sum_second, total_second, peak_second = second
    common = jnp.maximum(peak_first, peak_second)
    fade_first = jnp.exp(peak_first - common)
    fade_second = jnp.exp(peak_second - common)
    return (
        sum_first * fade_first[..., None] + sum_second * fade_second[..., None],
        total_first * fade_first + total_second * fade_second,
        common,
    )


def scan_mixer(
    mixer_input, mixer_gate, state_in, state_out, step_size, decay_log, skip_gain, prior_state
):
    tokens = mixer_input.shape[0]
    decay_rate = -jnp.exp(decay_log)
    log_fade = jnp.cumsum(step_size * decay_rate[None, :], axis=0)
    token_order = jnp.arange(tokens)
    causal_mask = token_order[:, None] >= token_order[None, :]
    fade_heads = jnp.transpose(log_fade)
    differ = fade_heads[:, :, None] - fade_heads[:, None, :]
    lower_fade = jnp.exp(jnp.where(causal_mask[None], differ, very_low))
    state_match = jnp.einsum("tn,sn->ts", state_out, state_in, preferred_element_type=jnp.float32)
    mixing = lower_fade * state_match[None]
    inputs_wide = mixer_input.astype(jnp.float32)
    scaled = step_size[:, :, None] * inputs_wide
    inner_part = jnp.einsum("hts,shp->thp", mixing, scaled, precision=lax.Precision.HIGHEST)
    carried = (
        jnp.einsum(
            "tn,hpn->thp",
            state_out.astype(jnp.float32),
            prior_state,
            precision=lax.Precision.HIGHEST,
        )
        * jnp.exp(log_fade)[:, :, None]
    )
    mixed_out = inner_part + carried + skip_gain[None, :, None] * inputs_wide
    return (mixed_out * jax.nn.silu(mixer_gate.astype(jnp.float32))).astype(jnp.bfloat16)


def general_form(
    residual,
    queries,
    incoming_keys,
    incoming_values,
    cache_keys,
    cached_value_rows,
    context,
    attention_out,
    mixer_input,
    mixer_gate,
    state_in,
    state_out,
    step_size,
    decay_log,
    skip_gain,
    prior_state,
    mixer_out,
    norm_gain,
    hidden_gate,
    hidden_up,
    hidden_down,
):
    tokens = queries.shape[0]
    head_depth = queries.shape[2]
    shared_heads = cache_keys.shape[1]
    group_width = queries.shape[1] // shared_heads
    local_span = cache_keys.shape[0]
    fresh_count = incoming_keys.shape[0]
    owner_index = lax.axis_index(("ctx", "row"))
    score_scale = 1.0 / math.sqrt(head_depth)
    query_view = queries.reshape(tokens, shared_heads, group_width, head_depth)
    block_size = min(512, local_span)
    blocks = local_span // block_size
    key_blocks = cache_keys.reshape(blocks, block_size, shared_heads, head_depth)
    value_blocks = cached_value_rows.reshape(blocks, block_size, shared_heads, head_depth)

    def visit_block(partial_state, inputs):
        block_keys, block_values, block_number = inputs
        scores = (
            jnp.einsum("tkgd,skd->kgts", query_view, block_keys, preferred_element_type=jnp.float32)
            * score_scale
        )
        position = owner_index * local_span + block_number * block_size + jnp.arange(block_size)
        visible = (position < context[0])[None, None, None, :]
        return (absorb(partial_state, scores, visible, block_values), None)

    start_state = (
        jnp.zeros((shared_heads, group_width, tokens, head_depth), jnp.float32),
        jnp.zeros((shared_heads, group_width, tokens), jnp.float32),
        jnp.full((shared_heads, group_width, tokens), very_low, jnp.float32),
    )
    partial_state = lax.scan(
        visit_block, start_state, (key_blocks, value_blocks, jnp.arange(blocks))
    )[0]
    fresh_scores = (
        jnp.einsum("tkgd,skd->kgts", query_view, incoming_keys, preferred_element_type=jnp.float32)
        * score_scale
    )
    source = owner_index * fresh_count + jnp.arange(fresh_count)
    fresh_visible = (source[None, :] <= jnp.arange(tokens)[:, None])[None, None]
    running_sum, weight_total, running_peak = absorb(
        partial_state, fresh_scores, fresh_visible, incoming_values
    )
    merged = combined_all((running_sum, weight_total, running_peak), ("ctx", "row"), join_partial)
    attended = (merged[0] / merged[1][..., None]).astype(jnp.bfloat16)
    attention_part = jnp.einsum(
        "kgtd,kgdc->tc",
        attended,
        attention_out.reshape(shared_heads, group_width, head_depth, -1),
        preferred_element_type=jnp.float32,
    )
    gated = scan_mixer(
        mixer_input, mixer_gate, state_in, state_out, step_size, decay_log, skip_gain, prior_state
    )
    mixer_rows = mixer_out.reshape(mixer_input.shape[1], -1, mixer_out.shape[1])
    mixer_part = jnp.einsum(
        "thp,hpc->tc",
        lax.all_gather(gated, ("ctx", "row"), axis=2, tiled=True),
        mixer_rows,
        preferred_element_type=jnp.float32,
    )
    branches = attention_part + mixer_part
    summed = lax.psum(branches, "head")
    combined = lax.all_to_all(summed, ("ctx", "row"), split_axis=0, concat_axis=1, tiled=True)
    trunk = (residual.astype(jnp.float32) + combined).astype(jnp.bfloat16)
    trunk_wide = trunk.astype(jnp.float32)
    inverse_rms = lax.rsqrt(jnp.mean(trunk_wide * trunk_wide, axis=1, keepdims=True) + 1e-05)
    normed = (trunk_wide * inverse_rms * norm_gain[None, :]).astype(jnp.bfloat16)
    column_count = hidden_gate.shape[0]
    column_start = lax.axis_index("head") * column_count
    normed_part = lax.dynamic_slice_in_dim(normed, column_start, column_count, 1)
    segment = lax.all_gather(normed_part, ("ctx", "row"), axis=0, tiled=True)
    pair_partial = jnp.stack(
        [
            jnp.dot(segment, hidden_gate, preferred_element_type=jnp.float32),
            jnp.dot(segment, hidden_up, preferred_element_type=jnp.float32),
        ]
    )
    pair_share = lax.psum_scatter(pair_partial, "head", scatter_dimension=1, tiled=True)
    hidden_share = (jax.nn.silu(pair_share[0]) * pair_share[1]).astype(jnp.bfloat16)
    hidden = lax.all_gather(hidden_share, "head", axis=0, tiled=True)
    down_rows = lax.psum_scatter(
        jnp.dot(hidden, hidden_down, preferred_element_type=jnp.float32),
        ("ctx", "row"),
        scatter_dimension=0,
        tiled=True,
    )
    trunk_part = lax.dynamic_slice_in_dim(trunk_wide, column_start, column_count, 1)
    return (trunk_part + down_rows).astype(jnp.bfloat16)


smem = pl.BlockSpec(memory_space=pltpu.SMEM)
whole = pl.BlockSpec(memory_space=pltpu.VMEM)


def local_call(kernel, outs, *args, scratch=(), cost=None, name=None):
    return pl.pallas_call(
        kernel,
        out_shape=tuple(jax.ShapeDtypeStruct(s, d) for s, d in outs),
        in_specs=[smem] + [whole] * (len(args) - 1),
        out_specs=tuple(whole for _ in outs),
        scratch_shapes=list(scratch),
        cost_estimate=cost,
        name=name,
    )(*args)


def wrap(x, n):
    return jnp.where(x >= n, x - n, x)


def split_three(x):
    high = x.astype(bf16).astype(f32)
    rest = x - high
    middle = rest.astype(bf16).astype(f32)
    return high, middle, rest - middle


def put_stats(table, head, peak, total):
    lane = lax.broadcasted_iota(jnp.int32, table.shape, 1) - 6 * head
    for i, piece in enumerate(split_three(peak) + split_three(total)):
        table = jnp.where(lane == i, piece, table)
    return table


def get_stats(table, head):
    at = 6 * head

    def three(a):
        return table[:, a : a + 1] + table[:, a + 1 : a + 2] + table[:, a + 2 : a + 3]

    return three(at), three(at + 3)


def attention_kernel(
    dims, sc, q, k, v, fresh_k, fresh_v, keep, send, keys, values, stats
):
    nc, nr, kv, width, span, fresh, scale2 = dims
    head = pl.program_id(0)
    heads = kv * width
    z, r, limit = sc[0], sc[1], sc[3]
    rows = nc * nr * fresh

    @pl.when(head == 0)
    def _():
        i = lax.broadcasted_iota(jnp.int32, (kv * lanes, kv * lanes), 0)
        j = lax.broadcasted_iota(jnp.int32, (kv * lanes, kv * lanes), 1)
        pick = ((i % lanes) * kv + i // lanes == j).astype(bf16)
        for source, target in ((k, keys), (v, values)):
            for b in range(span // lanes):
                part = jnp.dot(
                    pick, source[b * kv * lanes : (b + 1) * kv * lanes, :],
                    preferred_element_type=f32,
                ).astype(bf16)
                for g in range(kv):
                    target[g, b * lanes : (b + 1) * lanes, :] = part[g * lanes : (g + 1) * lanes]
        for source, target in ((fresh_k, keys), (fresh_v, values)):
            part = jnp.dot(
                pick[:, : kv * fresh], source[...], preferred_element_type=f32
            ).astype(bf16)
            for g in range(kv):
                target[g, span : span + lanes, :] = part[g * lanes : (g + 1) * lanes]
        stats[...] = jnp.zeros_like(stats)

    g = head // width
    query = jnp.concatenate(
        [q[0, wrap(z + a, nc) * nr + wrap(r + s, nr)] for s in range(nr) for a in range(nc)], axis=0
    )
    scores = lax.dot_general(
        query, keys[g], (((1,), (1,)), ((), ())), preferred_element_type=f32
    )
    cached, new = scores[:, :span], scores[:, span:]
    column = lax.broadcasted_iota(jnp.int32, (1, span), 1)
    cached = jnp.where(column < limit, cached, very_low)
    place = lax.broadcasted_iota(jnp.int32, (rows, lanes), 0)
    n = lax.broadcasted_iota(jnp.int32, (rows, lanes), 1)
    s, a, t = place // (nc * fresh), (place // fresh) % nc, place % fresh
    token = (wrap(z + a, nc) * nr + wrap(r + s, nr)) * fresh + t
    seen = (n < fresh) & ((z * nr + r) * fresh + n <= token)
    new = jnp.where(seen, new, very_low)
    peak = jnp.maximum(jnp.max(cached, axis=1, keepdims=True), jnp.max(new, axis=1, keepdims=True))
    peak = jnp.maximum(peak, lowest_peak)
    weights = jnp.exp2((cached - peak) * scale2)
    weights_new = jnp.exp2((new - peak) * scale2)
    total = jnp.sum(weights, axis=1, keepdims=True) + jnp.sum(weights_new, axis=1, keepdims=True)
    mixed = jnp.dot(weights.astype(bf16), values[g, :span, :], preferred_element_type=f32)
    mixed += jnp.dot(weights_new.astype(bf16), values[g, span:, :], preferred_element_type=f32)
    half = nc * fresh
    at = pl.multiple_of(head * lanes, lanes)
    mixed = mixed.astype(bf16)
    keep[:, pl.ds(at, lanes)] = mixed[:half]
    send[:, pl.ds(at, lanes)] = mixed[half:]
    stats[...] = put_stats(stats[...], head, peak * scale2, total)

    @pl.when(head == heads - 1)
    def _():
        keep[:, heads * lanes :] = stats[:half].astype(bf16)
        send[:, heads * lanes :] = stats[half:].astype(bf16)


def merge_parts(heads, parts, finish):
    tables = [p[:, heads * lanes :].astype(f32) for p in parts]
    for h in range(heads):
        stats = [get_stats(t, h) for t in tables]
        peak = functools.reduce(jnp.maximum, [m for m, _ in stats])
        fades = [jnp.exp2(m - peak) for m, _ in stats]
        mixed = sum(
            p[:, h * lanes : (h + 1) * lanes].astype(f32) * f for p, f in zip(parts, fades)
        )
        total = sum(l * f for (_, l), f in zip(stats, fades))
        finish(h, mixed, peak, total)


def merge_rows_kernel(dims, sc, mine, other, *outs):
    heads, nc, fresh = dims
    table = [jnp.zeros((nc * fresh, lanes), f32)]

    def finish(h, mixed, peak, total):
        mixed = mixed.astype(bf16)
        for a, out in enumerate(outs):
            out[:, h * lanes : (h + 1) * lanes] = mixed[a * fresh : (a + 1) * fresh]
        table[0] = put_stats(table[0], h, peak, total)

    merge_parts(heads, (mine, other), finish)
    packed = table[0].astype(bf16)
    for a, out in enumerate(outs):
        out[:, heads * lanes :] = packed[a * fresh : (a + 1) * fresh]


def merge_final_kernel(heads, sc, *refs):
    parts, out = refs[:-1], refs[-1]

    def finish(h, mixed, peak, total):
        out[:, h * lanes : (h + 1) * lanes] = (mixed / total).astype(bf16)

    merge_parts(heads, parts, finish)


def mixer_project_kernel(dims, sc, mine, other, weight, out, full):
    nc, nr, heads, channels = dims
    z, r = sc[0], sc[1]
    for s, source in enumerate((mine, other)):
        for a in range(nc):
            owner = wrap(z + a, nc) * nr + wrap(r + s, nr)
            for h in range(heads):
                at = pl.multiple_of(h * nc * nr * channels + owner * channels, channels)
                full[pl.ds(at, channels), :] = source[a, h * channels : (h + 1) * channels, :]
    out[...] = lax.dot_general(
        full[...], weight[...], (((0,), (0,)), ((), ())), preferred_element_type=f32
    )


def branch_kernel(dims, sc, mine, other, weight, mixer_part, keep, send):
    nc, nr, fresh = dims
    z, r = sc[0], sc[1]
    for s, (source, out) in enumerate(((mine, keep), (other, send))):
        attention = jnp.dot(source[...], weight[...], preferred_element_type=f32)
        for a in range(nc):
            block = wrap(z + a, nc) * nr + wrap(r + s, nr)
            at = pl.multiple_of(block * fresh, fresh)
            rows = attention[a * fresh : (a + 1) * fresh] + mixer_part[pl.ds(at, fresh), :]
            out[a * fresh : (a + 1) * fresh, :] = rows.astype(bf16)


def side_by_side_kernel(dims, sc, mine, other, *outs):
    fresh, columns = dims
    r = sc[1]
    for s, source in enumerate((mine, other)):
        at = pl.multiple_of(wrap(r + s, 2) * columns, lanes)
        for a, out in enumerate(outs):
            out[:, pl.ds(at, columns)] = source[a * fresh : (a + 1) * fresh, :]


def columns_kernel(dims, sc, *refs):
    nc, columns = dims
    z = sc[0]
    out = refs[-1]
    for a in range(nc):
        at = pl.multiple_of(wrap(z + nc - a, nc) * columns, lanes)
        out[:, pl.ds(at, columns)] = refs[a][...]


def trunk_kernel(columns, sc, residual, mine, other, gain, normed_part, trunk_part, normed, trunk):
    h = sc[2]
    total = residual[...].astype(f32) + (mine[...].astype(f32) + other[...].astype(f32))
    rounded = total.astype(bf16)
    trunk[...] = rounded
    wide = rounded.astype(f32)
    inverse = lax.rsqrt(jnp.mean(wide * wide, axis=1, keepdims=True) + 1e-05)
    normed[...] = (wide * inverse * gain[...]).astype(bf16)
    at = pl.multiple_of(h * columns, lanes)
    normed_part[...] = normed[:, pl.ds(at, columns)]
    trunk_part[...] = trunk[:, pl.ds(at, columns)]


def gate_up_kernel(unit, sc, mine, other, gate, up, keep, send, tokens):
    h = sc[2]
    half = mine.shape[0]

    @pl.when((pl.program_id(0) == 0) & (h == 0))
    def _():
        tokens[:half, :] = mine[...]
        tokens[half:, :] = other[...]

    @pl.when((pl.program_id(0) == 0) & (h != 0))
    def _():
        tokens[:half, :] = other[...]
        tokens[half:, :] = mine[...]

    for i, weight in enumerate((gate, up)):
        sums = jnp.dot(tokens[...], weight[...], preferred_element_type=f32)
        keep[i] = sums[:half]
        send[i] = sums[half:].astype(bf16)


def gate_up(sc, mine, other, gate, up, start, width, unit):
    half, depth = mine.shape
    first = start // unit
    steps = width // unit
    table = pl.BlockSpec((half, depth), lambda j: (0, 0))
    weight = pl.BlockSpec((depth, unit), lambda j: (0, first + j))
    out = pl.BlockSpec((2, half, unit), lambda j: (0, 0, j))
    return pl.pallas_call(
        functools.partial(gate_up_kernel, unit),
        grid=(steps,),
        out_shape=(
            jax.ShapeDtypeStruct((2, half, width), f32),
            jax.ShapeDtypeStruct((2, half, width), bf16),
        ),
        in_specs=[smem, table, table, weight, weight],
        out_specs=(out, out),
        scratch_shapes=[pltpu.VMEM((2 * half, depth), bf16)],
        cost_estimate=pl.CostEstimate(
            flops=8 * half * depth * width, transcendentals=0, bytes_accessed=4 * depth * width
        ),
        name="gate_up",
    )(sc, mine, other, gate, up)


def hidden_kernel(sc, mine, other, out):
    gate = mine[0] + other[0].astype(f32)
    up = mine[1] + other[1].astype(f32)
    out[...] = (gate / (1.0 + jnp.exp(-gate)) * up).astype(bf16)


def down_kernel(widths, first, last, sc, *refs):
    n = len(widths)
    mine, other, weight = refs[:n], refs[n : 2 * n], refs[2 * n]
    rest = refs[2 * n + 1 :]
    hidden = rest[-1]
    half = mine[0].shape[0]

    @pl.when(pl.program_id(0) == 0)
    def _():
        at = 0
        for m, o, w in zip(mine, other, widths):
            hidden[:half, at : at + w] = m[...]
            hidden[half:, at : at + w] = o[...]
            at += w

    sums = jnp.dot(hidden[...], weight[...], preferred_element_type=f32)
    if not first:
        sums += rest[0][...]
    if not last:
        rest[-2][...] = sums
        return
    keep, send = rest[-3], rest[-2]
    h = sc[2]

    @pl.when(h == 0)
    def _():
        keep[...] = sums[:half]
        send[...] = sums[half:].astype(bf16)

    @pl.when(h != 0)
    def _():
        keep[...] = sums[half:]
        send[...] = sums[:half].astype(bf16)


def down(sc, mine, other, weight, start, before, last):
    half = mine[0].shape[0]
    widths = tuple(m.shape[1] for m in mine)
    depth = sum(widths)
    columns = weight.shape[1]
    unit = 512 if columns % 512 == 0 else columns
    first = before is None
    hid = [pl.BlockSpec((half, w), lambda j: (0, 0)) for w in widths]
    both = pl.BlockSpec((2 * half, unit), lambda j: (0, j))
    one = pl.BlockSpec((half, unit), lambda j: (0, j))
    block = start // depth
    outs = (
        (jax.ShapeDtypeStruct((half, columns), f32), jax.ShapeDtypeStruct((half, columns), bf16))
        if last
        else jax.ShapeDtypeStruct((2 * half, columns), f32)
    )
    return pl.pallas_call(
        functools.partial(down_kernel, widths, first, last),
        grid=(columns // unit,),
        out_shape=outs,
        in_specs=[smem]
        + hid
        + hid
        + [pl.BlockSpec((depth, unit), lambda j: (block, j))]
        + ([] if first else [both]),
        out_specs=(one, one) if last else both,
        scratch_shapes=[pltpu.VMEM((2 * half, depth), bf16)],
        cost_estimate=pl.CostEstimate(
            flops=4 * half * depth * columns,
            transcendentals=0,
            bytes_accessed=2 * depth * columns + (0 if first else 8 * half * columns),
        ),
        name="down",
    )(sc, *mine, *other, weight, *([] if first else [before]))


def spread_kernel(fresh, sc, mine, other, own, *outs):
    own[...] = mine[:fresh] + other[:fresh].astype(f32)
    for a, out in enumerate(outs):
        rows = slice((a + 1) * fresh, (a + 2) * fresh)
        out[...] = (mine[rows] + other[rows].astype(f32)).astype(bf16)


def finish_kernel(sc, trunk, own, *refs):
    total = own[...]
    for part in refs[:-1]:
        total += part[...].astype(f32)
    refs[-1][...] = (trunk[...].astype(f32) + total).astype(bf16)


def small_form(
    nc,
    nr,
    nh,
    residual,
    queries,
    incoming_keys,
    incoming_values,
    cache_keys,
    cached_value_rows,
    context,
    attention_out,
    mixer_input,
    mixer_gate,
    state_in,
    state_out,
    step_size,
    decay_log,
    skip_gain,
    prior_state,
    mixer_out,
    norm_gain,
    hidden_gate,
    hidden_up,
    hidden_down,
):
    tokens, heads, depth = queries.shape
    span, kv = cache_keys.shape[:2]
    fresh = incoming_keys.shape[0]
    half = nc * fresh
    width = heads // kv
    z, r, h = lax.axis_index("ctx"), lax.axis_index("row"), lax.axis_index("head")
    limit = context[0] - (z * nr + r) * span
    sc = jnp.stack([z, r, h, limit]).astype(jnp.int32)

    def shift(x, by):
        return lax.ppermute(x, "ctx", [(i, (i + by) % nc) for i in range(nc)])

    def to_owners(parts):
        return [parts[0]] + [shift(parts[a], a) for a in range(1, nc)]

    def from_all(x):
        return [x] + [shift(x, -a) for a in range(1, nc)]

    def other_row(x):
        return lax.ppermute(x, "row", [(i, (i + 1) % nr) for i in range(nr)])

    def other_head(x):
        return lax.ppermute(x, "head", [(i, (i + 1) % nh) for i in range(nh)])

    gated = scan_mixer(
        mixer_input, mixer_gate, state_in, state_out, step_size, decay_log, skip_gain, prior_state
    )
    state_heads, channels = gated.shape[1:]
    gated = jnp.transpose(gated, (1, 2, 0)).reshape(state_heads * channels, tokens)
    gated_all = jnp.stack(from_all(gated))
    gated_other = other_row(gated_all)

    dims = (nc, nr, kv, width, span, fresh, math.log2(math.e) / math.sqrt(depth))
    wide = (heads + 1) * lanes
    query_view = jnp.transpose(queries, (1, 0, 2)).reshape(heads, nc * nr, fresh, depth)
    fixed = lambda shape: pl.BlockSpec(shape, lambda i: (0,) * len(shape))
    keep, send = pl.pallas_call(
        functools.partial(attention_kernel, dims),
        grid=(heads,),
        out_shape=(jax.ShapeDtypeStruct((half, wide), bf16),) * 2,
        in_specs=[
            smem,
            pl.BlockSpec((1, nc * nr, fresh, depth), lambda i: (i, 0, 0, 0)),
            fixed((span * kv, depth)),
            fixed((span * kv, depth)),
            fixed((fresh * kv, depth)),
            fixed((fresh * kv, depth)),
        ],
        out_specs=(fixed((half, wide)),) * 2,
        scratch_shapes=[
            pltpu.VMEM((kv, span + lanes, depth), bf16),
            pltpu.VMEM((kv, span + lanes, depth), bf16),
            pltpu.VMEM((tokens, lanes), f32),
        ],
        cost_estimate=pl.CostEstimate(
            flops=4 * tokens * heads * span * depth,
            transcendentals=tokens * heads * span,
            bytes_accessed=4 * span * kv * depth,
        ),
        name="attention",
    )(
        sc,
        query_view,
        cache_keys.reshape(span * kv, depth),
        cached_value_rows.reshape(span * kv, depth),
        incoming_keys.reshape(fresh * kv, depth),
        incoming_values.reshape(fresh * kv, depth),
    )
    parts = local_call(
        functools.partial(merge_rows_kernel, (heads, nc, fresh)),
        [((fresh, wide), bf16)] * nc,
        sc,
        keep,
        other_row(send),
        name="merge_rows",
    )
    (attended,) = local_call(
        functools.partial(merge_final_kernel, heads),
        [((fresh, heads * lanes), bf16)],
        sc,
        *to_owners(parts),
        name="merge_final",
    )
    (mixer_part,) = local_call(
        functools.partial(mixer_project_kernel, (nc, nr, state_heads, channels)),
        [((tokens, mixer_out.shape[1]), f32)],
        sc,
        gated_all,
        gated_other,
        mixer_out,
        scratch=[pltpu.VMEM((state_heads * channels * nc * nr, tokens), bf16)],
        name="mixer_project",
    )
    attended_all = jnp.concatenate(from_all(attended), axis=0)
    columns = attention_out.shape[1]
    keep, send = local_call(
        functools.partial(branch_kernel, (nc, nr, fresh)),
        [((half, columns), bf16)] * 2,
        sc,
        attended_all,
        other_row(attended_all),
        attention_out,
        mixer_part,
        name="branches",
    )
    parts = local_call(
        functools.partial(side_by_side_kernel, (fresh, columns)),
        [((fresh, nr * columns), bf16)] * nc,
        sc,
        keep,
        other_row(send),
        name="side_by_side",
    )
    model = residual.shape[1]
    (branches,) = local_call(
        functools.partial(columns_kernel, (nc, nr * columns)),
        [((fresh, model), bf16)],
        sc,
        *to_owners(parts),
        name="columns",
    )
    depth_in = hidden_gate.shape[0]
    normed, trunk = local_call(
        functools.partial(trunk_kernel, depth_in),
        [((fresh, depth_in), bf16)] * 2,
        sc,
        residual,
        branches,
        other_head(branches),
        norm_gain.reshape(1, model),
        scratch=[pltpu.VMEM((fresh, model), bf16)] * 2,
        name="trunk",
    )
    normed_all = jnp.concatenate(from_all(normed), axis=0)
    normed_other = other_row(normed_all)

    count = hidden_gate.shape[1]
    unit = 3 * lanes
    units = count // unit
    sizes = [1] + [2] * ((units - 3) // 2) + [1] * (2 + (units - 3) % 2)
    start = 0
    mine, theirs = [], []
    for size in sizes:
        w = size * unit
        kept, sent = gate_up(sc, normed_all, normed_other, hidden_gate, hidden_up, start, w, unit)
        (hidden,) = local_call(
            hidden_kernel, [((half, w), bf16)], sc, kept, other_head(sent), name="hidden"
        )
        mine.append(hidden)
        theirs.append(other_head(hidden))
        start += w
    tail = sizes[-1] * unit
    sums = down(sc, mine[:-1], theirs[:-1], hidden_down, 0, None, False)
    keep, send = down(sc, mine[-1:], theirs[-1:], hidden_down, start - tail, sums, True)
    own, *parts = local_call(
        functools.partial(spread_kernel, fresh),
        [((fresh, depth_in), f32)] + [((fresh, depth_in), bf16)] * (nc - 1),
        sc,
        keep,
        other_row(send),
        name="spread",
    )
    received = [shift(part, a + 1) for a, part in enumerate(parts)]
    (out,) = local_call(
        finish_kernel, [((fresh, depth_in), bf16)], sc, trunk, own, *received, name="finish"
    )
    return out


def fits_small(mesh, args):
    return mesh.shape["row"] == 2 and mesh.shape["head"] == 2 and mesh.shape["ctx"] <= 4


def solution(mesh):
    in_specs = (
        P(("groups", "ctx", "row"), None),
        P("groups", "head", None),
        P(("groups", "ctx", "row"), "head", None),
        P(("groups", "ctx", "row"), "head", None),
        P(("groups", "ctx", "row"), "head", None),
        P(("groups", "ctx", "row"), "head", None),
        P("groups"),
        P("head", ("ctx", "row")),
        P("groups", "head", ("ctx", "row")),
        P("groups", "head", ("ctx", "row")),
        P("groups", None),
        P("groups", None),
        P("groups", "head"),
        P("head"),
        P("head"),
        P(("groups", "head"), ("ctx", "row"), None),
        P("head", ("ctx", "row")),
        P(),
        P("head", ("ctx", "row")),
        P("head", ("ctx", "row")),
        P(("ctx", "row"), "head"),
    )
    out_specs = P(("groups", "ctx", "row"), "head")
    nc, nr, nh = mesh.shape["ctx"], mesh.shape["row"], mesh.shape["head"]

    def on_device(*args):
        if fits_small(mesh, args):
            return small_form(nc, nr, nh, *args)
        return general_form(*args)

    return jax.shard_map(
        on_device, mesh=mesh, in_specs=in_specs, out_specs=out_specs, check_vma=False
    )
```
